256 devices in a mesh: grp: 8 (over x, core), row: 32 (over z, y).
Axes of the slice: x: 4, y: 4, z: 8, core: 2. Of those that a mesh axis runs over, the one named last changes fastest.
Arguments:
- placing: int32 [8192], P('grp'), parts along dimension 0, may hold values from 0 to 1023, as said below
- lengths: int32 [512], P('grp'), parts along dimension 0, may hold values from 1 to 48, 1024 in all
- diag_blocks: float32 [8192, 128, 128], P(('grp', 'row')), parts along dimension 0, as said below
- lower_blocks: float32 [8192, 128, 128], P(('grp', 'row')), parts along dimension 0, may hold values from -0.25 to 0.25
- right_side: float32 [8192, 128, 128], P(('grp', 'row')), parts along dimension 0, may hold values from -6 to 6
Outputs:
- solution: float32 [8192, 128, 128], P(('grp', 'row')), parts along dimension 0
- residual: float32 [8192, 128, 128], P(('grp', 'row')), parts along dimension 0
The draws below stay inside these ranges and needn't reach their ends.
There are 8 independent parts, one for each index of `grp`. The reference program is written for one: setup_inputs(seed, part) draws one part's arguments, and reference() takes and returns one part's arrays. A program takes and returns all parts, laid end to end along the dimension named above; each array names one. Nothing has to cross between parts.
Inputs may be any that keep to these rules, and one draw needn't show every extreme that they name: `placing`: A permutation of 0 .. 1023. Device d holds the slots d * 32 .. (d + 1) * 32 - 1, and among them exactly 1 name block rows of each range e * 32 .. (e + 1) * 32 - 1. `lengths`: they sum to 1024. `diag_blocks`: every block is symmetric, and the assembled operator of every system is positive definite.
All inputs are finite; a program needn't handle non-finite values.
Results may differ from the reference program's by a relative error of at most 0.0003.
Values sent between devices are 32-bit elements; how exact they have to be, the bound alone decides.
A program may use at most 128 MiB of HBM per device.

```python
import math
import jax
import jax.numpy as jnp
import numpy as np
from jax import lax

B = 128
K = 128
BPD = 32
ITERS = 4
NB = 1024
SYSTEMS = 64
MOSTLEN = 48


def shuffle_one(subkey):
    return jax.random.permutation(subkey, BPD)


def draw_placing(key, part):
    groups = NB // BPD
    share_rows = BPD // groups
    first_key, second_key = jax.random.split(jax.random.fold_in(key, 11))
    shuffled = jax.vmap(shuffle_one)(jax.random.split(first_key, groups)).astype(jnp.int32)
    owned = shuffled + (jnp.arange(groups, dtype=jnp.int32) * BPD)[:, None]
    spread_out = owned.reshape(groups, groups, share_rows).transpose(1, 0, 2).reshape(groups, BPD)
    mixing = jax.vmap(shuffle_one)(jax.random.split(second_key, groups)).astype(jnp.int32)
    return jnp.take_along_axis(spread_out, mixing, axis=1).reshape(NB).astype(jnp.int32)


def draw_diag_blocks(key, part):
    first_key, second_key = jax.random.split(jax.random.fold_in(key, 23))
    raw_part = jax.random.normal(first_key, (NB, B, B), jnp.float32) * (0.5 / B ** 0.5)
    shifts = jax.random.uniform(second_key, (NB,), jnp.float32, 5.0, 10.0)
    identity = jnp.eye(B, dtype=jnp.float32)
    blocks = raw_part + jnp.swapaxes(raw_part, 1, 2) + shifts[:, None, None] * identity[None, :, :]
    return blocks.astype(jnp.float32)


def block_scale(rng, extent, cuts, low, high):
    loudness = 1.0
    for dim, blocks in cuts:
        draws = jax.random.uniform(jax.random.fold_in(jax.random.fold_in(rng, 6), dim), (blocks,), jnp.float32, low / len(cuts), high / len(cuts))
        loudness = loudness * jnp.repeat(jnp.exp(draws), extent[dim] // blocks).reshape((-1,) + (1,) * (len(extent) - 1 - dim))
    return loudness


def length_profile(amount, total, most, lean):
    loads = [(1 << 20) // math.isqrt(rank ** lean) + 1 for rank in range(2, amount + 1)]
    surplus, holding = total - most - (amount - 1), [1] * (amount - 1)
    while surplus > 0:
        free = [i for i in range(amount - 1) if holding[i] < most]
        whole, left = sum([loads[i] for i in free]), surplus
        for i in free:
            extra = min(most - holding[i], max(1, left * loads[i] // whole), surplus)
            holding[i] = holding[i] + extra
            surplus = surplus - extra
    return np.array([most] + holding)


def uneven_parts(rng, number_of, total, reach, lean):
    if number_of == 2:
        one = jax.random.randint(rng, (), max(1, total - reach), min(reach, total - 1) + 1)
        return jnp.stack([one, total - one])
    tallies = jnp.asarray(length_profile(number_of, total, reach, lean), jnp.int32)
    pairs = (number_of - 1) // 2
    giver, taker = tallies[1:1 + 2 * pairs:2], tallies[2:2 + 2 * pairs:2]
    slack = jnp.minimum(giver - 1, reach - taker)
    shifted = jax.random.randint(jax.random.fold_in(rng, 1), (pairs,), 0, 1 << 20) % (slack + 1)
    tallies = tallies.at[1:1 + 2 * pairs:2].set(giver - shifted).at[2:2 + 2 * pairs:2].set(taker + shifted)
    return tallies[jax.random.permutation(jax.random.fold_in(rng, 2), number_of)]


def bell_draw(key, shape, deviation, most, cuts=(), held_as=jnp.bfloat16):
    array = jax.random.normal(key, shape, jnp.float32) * deviation
    if len(cuts) > 0:
        array = block_scale(key, shape, cuts, -0.22, 0.18) * array
    return jnp.clip(array, min=-most, max=most).astype(held_as)


def setup_inputs(seed: int = 0, part: int = 0) -> dict:
    streams_of = jax.random.split(jax.random.key(seed), 6)
    own_keys = jax.random.split(jax.random.fold_in(streams_of[5], part), 6)
    return {
        "placing": draw_placing(jax.random.fold_in(jax.random.fold_in(streams_of[5], part), 71), part),
        "lengths": uneven_parts(own_keys[1], SYSTEMS, NB, MOSTLEN, 2).astype(jnp.int32),
        "diag_blocks": draw_diag_blocks(jax.random.fold_in(jax.random.fold_in(streams_of[5], part), 71), part),
        "lower_blocks": bell_draw(own_keys[3], (NB, B, B), (4 * B) ** -0.5, 0.25, ((0, 32),), jnp.float32),
        "right_side": bell_draw(own_keys[4], (NB, B, K), 1.0, 6.0, ((0, 32),), jnp.float32),
    }


HIGHEST = lax.Precision.HIGHEST


def reference(placing, lengths, diag_blocks, lower_blocks, right_side):
    inverse = jnp.argsort(placing, stable=True).astype(jnp.int32)
    diagonal = diag_blocks[inverse]
    coupling_raw = lower_blocks[inverse]
    rhs_nat = right_side[inverse]
    seg_ends = jnp.cumsum(lengths).astype(jnp.int32)
    starts = seg_ends - lengths
    global_rows = jnp.arange(NB, dtype=jnp.int32)
    segment = jnp.sum((global_rows[:, None] >= seg_ends[None, :]).astype(jnp.int32), axis=1).astype(jnp.int32)
    is_first = jnp.any(global_rows[:, None] == starts[None, :], axis=1)
    keep_mask = jnp.where(is_first, 0.0, 1.0).astype(jnp.float32)
    coupling_low = coupling_raw * keep_mask[:, None, None]

    def operate(field):
        center = jnp.einsum('jab,jbk->jak', diagonal, field, precision=HIGHEST)
        shifted_down = jnp.concatenate([jnp.zeros_like(field[:1]), field[:-1]], axis=0)
        from_below = jnp.einsum('jab,jbk->jak', coupling_low, shifted_down, precision=HIGHEST)
        turned = jnp.einsum('jba,jbk->jak', coupling_low, field, precision=HIGHEST)
        from_above = jnp.concatenate([turned[1:], jnp.zeros_like(turned[:1])], axis=0)
        return center + from_below + from_above

    def per_system(values):
        return jax.ops.segment_sum(jnp.sum(values, axis=1), segment, num_segments=SYSTEMS)

    def spread(coefficient):
        return coefficient[segment][:, None, :]

    solution = jnp.zeros_like(rhs_nat)
    residual = rhs_nat
    direction = rhs_nat
    norm_now = per_system(residual * residual)
    for iteration in range(ITERS):
        image = operate(direction)
        step_size = norm_now / per_system(direction * image)
        solution = solution + spread(step_size) * direction
        residual = residual - spread(step_size) * image
        norm_next = per_system(residual * residual)
        direction = residual + spread(norm_next / norm_now) * direction
        norm_now = norm_next
    return solution, residual
```

```python
import functools

import jax
import jax.numpy as jnp
from jax import lax
from jax.experimental import pallas as pl
from jax.experimental.pallas import tpu as pltpu
from jax.sharding import PartitionSpec as P

ITERS = 4
NZ, NY = 8, 4
N = NZ * NY
BPD = 32
B = 128
H = B // 2
SYSTEMS = 64
DROWS = H + 8
CHUNKS = 4
F32, BF16 = jnp.float32, jnp.bfloat16
HIGHEST = lax.Precision.HIGHEST
MESH = pl.DeviceIdType.MESH


def iota(shape, dim):
    return lax.broadcasted_iota(jnp.int32, shape, dim)


def halves(v):
    hi = v.astype(BF16)
    return hi, (v - hi.astype(F32)).astype(BF16)


def side(v):
    return jnp.concatenate(halves(v), axis=1)


def times(left, right):
    out = jnp.dot(left, jnp.concatenate([right, right], axis=0), preferred_element_type=F32)
    return out[:, :B] + out[:, B:]


def triangle_of(block):
    top, bottom = block[:H], block[H:]
    row, lane = iota((H, B), 0), iota((H, B), 1)
    turned = pltpu.roll(bottom, H, 1)
    body = jnp.where((lane < H) & (row > lane), turned, top)
    diagonal = jnp.sum(jnp.where(row + H == lane, bottom, 0.0), axis=0, keepdims=True)
    return body, diagonal


def whole_of(body, diagonal):
    row, lane = iota((H, B), 0), iota((H, B), 1)
    low = jnp.where(row + H == lane, diagonal, pltpu.roll(body, H, 1))
    known = jnp.concatenate([body, low], axis=0)
    row, lane = iota((B, B), 0), iota((B, B), 1)
    top = row < H
    mask = (top & (lane >= row)) | (~top & (lane >= H) & (lane <= row))
    return jnp.where(mask, known, known.T)


def kernel(
    table, lengths, rhs_hbm, diag_hbm, low_hbm, x_hbm, r_hbm,
    st_f, st_d, st_l, sd_f, sd_d, sd_l, rc_f, rc_d, rc_l,
    w_d, w_t, w_l, x, r, p, s, im, rw, ss_rows, keep, near, alpha, beta,
    halo_p, halo_t, turned, part, parts, x_out, r_out,
    in_sem, a2a_send, a2a_recv, halo_send, halo_recv, part_send, part_recv, out_sem,
):
    me = lax.axis_index("row")
    z, y = me // NY, me % NY

    def away(i, way):
        dy, k = i // NZ, i % NZ
        dz = ((k + 1) // 2) * (2 * (k % 2) - 1)
        return ((z + way * dz + NZ) % NZ) * NY + (y + way * dy + NY) % NY

    def slot_of(t):
        return table[t]

    def row_of(d):
        return table[N + d]

    def src_of(l):
        return table[2 * N + l]

    barrier = pltpu.get_barrier_semaphore()

    def greet(i, carry):
        pl.semaphore_signal(barrier, 1, device_id={"row": away(i, 1)}, device_id_type=MESH)
        return carry

    def sent(phase, i, src, dst):
        t = away(i, 1)
        return pltpu.make_async_remote_copy(
            src.at[t], dst.at[me], a2a_send.at[phase, i], a2a_recv.at[phase, i],
            device_id={"row": t}, device_id_type=MESH,
        )

    def arriving(phase, i, src, dst):
        d = away(i, -1)
        return pltpu.make_async_remote_copy(
            src.at[d], dst.at[d], a2a_send.at[phase, i], a2a_recv.at[phase, i],
            device_id={"row": d}, device_id_type=MESH,
        )

    phases = ((sd_l, rc_l), (sd_d, rc_d), (sd_f, rc_f))
    owns = [
        pltpu.make_async_copy(src.at[me], dst.at[me], in_sem.at[3 + k]) for k, (src, dst) in enumerate(phases)
    ]

    def send_all(phase):
        src, dst = phases[phase]

        def start(i, carry):
            sent(phase, i, src, dst).start()
            return carry

        lax.fori_loop(1, N, start, 0)
        owns[phase].start()

    def receive_all(phase):
        src, dst = phases[phase]

        def wait(i, carry):
            arriving(phase, i, src, dst).wait_recv()
            return carry

        lax.fori_loop(1, N, wait, 0)
        owns[phase].wait()

    loads = [
        pltpu.make_async_copy(src, dst, in_sem.at[k])
        for k, (src, dst) in enumerate(((low_hbm, st_l), (diag_hbm, st_d), (rhs_hbm, st_f)))
    ]
    lax.fori_loop(1, N, greet, 0)
    for load in loads:
        load.start()
    loads[0].wait()

    def gather_l(t, carry):
        sd_l[t] = st_l[slot_of(t)]
        return carry

    def gather_d(t, carry):
        body, diagonal = triangle_of(st_d[slot_of(t)])
        sd_d[t, 0:H] = body
        sd_d[t, H:DROWS] = jnp.broadcast_to(diagonal, (8, B))
        return carry

    def gather_f(t, carry):
        sd_f[t] = st_f[slot_of(t)]
        return carry

    lax.fori_loop(0, N, gather_l, 0)
    pl.semaphore_wait(barrier, N - 1)
    send_all(0)
    loads[1].wait()
    lax.fori_loop(0, N, gather_d, 0)
    send_all(1)
    loads[2].wait()
    lax.fori_loop(0, N, gather_f, 0)
    send_all(2)

    base = me * BPD
    rows = iota((BPD, B), 0) + base
    lane = iota((BPD, B), 1)
    eighths = base + iota((BPD, 8 * BPD), 1) // 8
    cols = jnp.full((BPD, B), -1, jnp.int32)
    for k, j in enumerate((base - 1, base - BPD - 1, base + BPD, base + 2 * BPD)):
        cols = jnp.where(lane == k, j, cols)

    def count(q, carry):
        end, a, b, c, e = carry
        end = end + lengths[q]
        one = lambda m: jnp.where(m, 1, 0)
        return (
            end, a + one(rows >= end), b + one(cols >= end), c + one(rows - 1 >= end), e + one(eighths >= end),
        )

    zero = jnp.zeros((BPD, B), jnp.int32)
    _, seg, seg_cols, seg_before, seg_eighths = lax.fori_loop(
        0, SYSTEMS, count, (jnp.int32(0), zero, zero, zero, jnp.zeros((BPD, 8 * BPD), jnp.int32))
    )
    keep[...] = jnp.where((seg != seg_before) | (rows == 0), 0.0, 1.0)
    same = jnp.where((seg == seg_cols) & (cols >= 0), 1.0, 0.0).astype(F32)
    for k in range(4):
        near[k] = jnp.broadcast_to(same[:, k : k + 1], (BPD, B))
    same_here = jnp.where(jnp.concatenate([seg, seg], axis=1) == seg_eighths, 1.0, 0.0).astype(F32)

    receive_all(0)

    def open_l(d, carry):
        v = rc_l[d] * keep[pl.ds(row_of(d), 1)]
        w_l[d] = side(v)
        w_t[d] = side(v.T)
        return carry

    lax.fori_loop(0, N, open_l, 0)
    receive_all(1)

    def open_d(d, carry):
        w_d[d] = side(whole_of(rc_d[d, 0:H], rc_d[d, H : H + 1]))
        return carry

    lax.fori_loop(0, N, open_d, 0)
    receive_all(2)

    def settle(l, carry):
        v = rc_f[src_of(l)]
        r[l] = v
        rw[l] = side(v)
        return carry

    lax.fori_loop(0, BPD, settle, 0)

    def shift(by):
        return (me + by + N) % N

    def remote(src, dst, send, recv, by):
        return pltpu.make_async_remote_copy(
            src, dst, send, recv, device_id={"row": shift(by)}, device_id_type=MESH
        )

    def multiply(it):
        down = remote(r.at[BPD - 1], halo_p.at[it], halo_send.at[it, 0], halo_recv.at[it, 0], 1)
        up = remote(turned.at[it], halo_t.at[it], halo_send.at[it, 1], halo_recv.at[it, 1], -1)
        down.start()

        def products(j, last=False):
            here = src_of(j)
            mats = [w_t[here], w_d[here]]
            if not last:
                mats.append(w_l[src_of(j + 1)])
            out = times(jnp.concatenate(mats, axis=0), rw[j])
            return [out[k * B : (k + 1) * B] for k in range(len(mats))]

        t, c, b = products(0)
        turned[it] = t
        up.start()
        im[0] = c
        im[1] = b

        def step(j, carry):
            t, c, b = products(j)
            im[j - 1] = im[j - 1] + t
            im[j] = im[j] + c
            im[j + 1] = b
            return carry

        lax.fori_loop(1, BPD - 1, step, 0)
        t, c = products(BPD - 1, last=True)
        im[BPD - 2] = im[BPD - 2] + t
        im[BPD - 1] = im[BPD - 1] + c
        down.wait_recv()
        im[0] = im[0] + times(w_l[src_of(0)], side(halo_p[it]))
        up.wait_recv()
        im[BPD - 1] = im[BPD - 1] + halo_t[it]
        down.wait_send()
        up.wait_send()

    def two_sums(it):
        def row_sums(l, carry):
            v = r[l]
            at = pl.ds(pl.multiple_of(8 * l, 8), 8)
            ss_rows[at, 0:B] = jnp.sum((v * v).reshape(B // 8, 8, B), axis=0)
            ss_rows[at, B : 2 * B] = jnp.sum((v * im[l]).reshape(B // 8, 8, B), axis=0)
            return carry

        lax.fori_loop(0, BPD, row_sums, 0)
        local = jnp.dot(same_here, ss_rows[...], precision=HIGHEST, preferred_element_type=F32)
        for k, row in enumerate((0, BPD - 1)):
            part[it, k, 0:1] = local[row : row + 1, :B]
            part[it, k, 1:2] = local[row : row + 1, B:]
        copies = [
            remote(part.at[it, k], parts.at[it, q], part_send.at[it, q], part_recv.at[it, q], by)
            for q, (k, by) in enumerate(((1, 1), (1, 2), (0, -1), (0, -2)))
        ]
        for copy in copies:
            copy.start()
        first, second = local[:, :B], local[:, B:]
        for copy in copies:
            copy.wait_recv()
            copy.wait_send()
        for q in range(4):
            first = first + near[q] * parts[it, q, 0:1]
            second = second + near[q] * parts[it, q, 1:2]
        return first, second

    for it in range(ITERS):
        multiply(it)
        norm, product = two_sums(it)
        if it == 0:
            step_size = norm / product
        else:
            ratio = norm / norm_before
            step_size = norm / (product - ratio * norm / step_size)
            beta[...] = ratio
        alpha[...] = step_size
        norm_before = norm

        def update(l, carry, it=it):
            a = alpha[pl.ds(l, 1)]
            res, image = r[l], im[l]
            if it == 0:
                direction, along = res, image
                x[l] = a * direction
            else:
                b = beta[pl.ds(l, 1)]
                direction = res + b * p[l]
                along = image + b * s[l]
                x[l] = x[l] + a * direction
            res = res - a * along
            r[l] = res
            p[l] = direction
            s[l] = along
            rw[l] = side(res)
            return carry

        if it + 1 < ITERS:
            lax.fori_loop(0, BPD, update, 0)

    outs = []
    span = BPD // CHUNKS
    for c in range(CHUNKS):
        def finish(q, carry, c=c):
            l = c * span + q
            a = alpha[pl.ds(l, 1)]
            res, image = r[l], im[l]
            b = beta[pl.ds(l, 1)]
            x_out[c][q] = x[l] + a * (res + b * p[l])
            r_out[c][q] = res - a * (image + b * s[l])
            return carry

        lax.fori_loop(0, span, finish, 0)
        for k, (src, dst) in enumerate(((x_out, x_hbm), (r_out, r_hbm))):
            outs.append(pltpu.make_async_copy(src[c], dst.at[pl.ds(c * span, span)], out_sem.at[c, k]))
            outs[-1].start()

    def drained(i, carry):
        for phase, (src, dst) in enumerate(phases):
            sent(phase, i, src, dst).wait_send()
        return carry

    lax.fori_loop(1, N, drained, 0)
    for out in outs:
        out.wait()


def body(placing, lengths, diag_blocks, lower_blocks, right_side):
    me = lax.axis_index("row")
    slots = placing.reshape(N, BPD)
    owner, local = slots // BPD, slots % BPD
    index = jnp.arange(BPD, dtype=jnp.int32)
    own = lax.dynamic_slice_in_dim(owner, me, 1, 0)
    slot_of = jnp.sum(jnp.where(own == index[:, None], index[None, :], 0), axis=1)
    row_of = jnp.sum(jnp.where(owner == me, local, 0), axis=1)
    src_of = jnp.sum(
        jnp.where((owner == me) & (local == index[:, None, None]), index[None, :, None], 0), axis=(1, 2)
    )
    table = jnp.concatenate([slot_of, row_of, src_of]).astype(jnp.int32)
    field = jax.ShapeDtypeStruct((BPD, B, B), F32)
    smem, hbm = pl.BlockSpec(memory_space=pltpu.SMEM), pl.BlockSpec(memory_space=pl.ANY)
    blocks = pltpu.VMEM((BPD, B, B), F32)
    packed = pltpu.VMEM((BPD, DROWS, B), F32)
    pairs = pltpu.VMEM((BPD, B, 2 * B), BF16)
    lines = pltpu.VMEM((BPD, B), F32)
    halo = pltpu.VMEM((ITERS, B, B), F32)
    dma = pltpu.SemaphoreType.DMA
    return pl.pallas_call(
        kernel,
        out_shape=(field, field),
        in_specs=[smem, smem, hbm, hbm, hbm],
        out_specs=(hbm, hbm),
        scratch_shapes=[blocks] * 3 + [blocks, packed, blocks] * 2 + [pairs] * 3 + [blocks] * 5 + [pairs]
        + [pltpu.VMEM((8 * BPD, 2 * B), F32), lines, pltpu.VMEM((4, BPD, B), F32), lines, lines]
        + [halo] * 3 + [pltpu.VMEM((ITERS, 2, 8, B), F32), pltpu.VMEM((ITERS, 4, 8, B), F32)]
        + [(pltpu.VMEM((BPD // CHUNKS, B, B), F32),) * CHUNKS] * 2
        + [dma((6,)), dma((3, N)), dma((3, N)), dma((ITERS, 2)), dma((ITERS, 2)), dma((ITERS, 4)), dma((ITERS, 4)), dma((CHUNKS, 2))],
        compiler_params=pltpu.CompilerParams(
            collective_id=0, has_side_effects=True, vmem_limit_bytes=60 * 1024 * 1024
        ),
    )(table, lengths, right_side, diag_blocks, lower_blocks)


def solution(mesh):
    blocks = P(("grp", "row"), None, None)
    return jax.shard_map(
        body,
        mesh=mesh,
        in_specs=(P("grp"), P("grp"), blocks, blocks, blocks),
        out_specs=(blocks, blocks),
        check_vma=False,
    )
```

```python
import functools

import jax
import jax.numpy as jnp
from jax import lax
from jax.experimental import pallas as pl
from jax.experimental.pallas import tpu as pltpu
from jax.sharding import PartitionSpec as P

ITERS = 4
NZ, NY = 8, 4
N = NZ * NY
BPD = 32
B = 128
H = B // 2
SYSTEMS = 64
DROWS = H + 8
CHUNKS = 4
F32, BF16 = jnp.float32, jnp.bfloat16
HIGHEST = lax.Precision.HIGHEST
MESH = pl.DeviceIdType.MESH


def iota(shape, dim):
    return lax.broadcasted_iota(jnp.int32, shape, dim)


def halves(v):
    hi = v.astype(BF16)
    return hi, (v - hi.astype(F32)).astype(BF16)


def side(v):
    return jnp.concatenate(halves(v), axis=1)


def times(left, right):
    out = jnp.dot(left, jnp.concatenate([right, right], axis=0), preferred_element_type=F32)
    return out[:, :B] + out[:, B:]


def triangle_of(block):
    top, bottom = block[:H], block[H:]
    row, lane = iota((H, B), 0), iota((H, B), 1)
    turned = pltpu.roll(bottom, H, 1)
    body = jnp.where((lane < H) & (row > lane), turned, top)
    diagonal = jnp.sum(jnp.where(row + H == lane, bottom, 0.0), axis=0, keepdims=True)
    return body, diagonal


def whole_of(body, diagonal):
    row, lane = iota((H, B), 0), iota((H, B), 1)
    low = jnp.where(row + H == lane, diagonal, pltpu.roll(body, H, 1))
    known = jnp.concatenate([body, low], axis=0)
    row, lane = iota((B, B), 0), iota((B, B), 1)
    top = row < H
    mask = (top & (lane >= row)) | (~top & (lane >= H) & (lane <= row))
    return jnp.where(mask, known, known.T)


def kernel(
    table, lengths, rhs_hbm, diag_hbm, low_hbm, x_hbm, r_hbm,
    st_f, st_d, st_l, sd_f, sd_d, sd_l, rc_f, rc_d, rc_l,
    w_d, w_t, w_l, x, r, p, s, im, rw, ss_rows, keep, near, alpha, beta,
    ends_f, ends_im, ends_r, ends_s, ends_rw, first_l, next_l, w_n, part, parts, x_out, r_out,
    in_sem, a2a_send, a2a_recv, halo_send, halo_recv, part_send, part_recv, out_sem,
):
    me = lax.axis_index("row")
    z, y = me // NY, me % NY

    def away(i, way):
        dy, k = i // NZ, i % NZ
        dz = ((k + 1) // 2) * (2 * (k % 2) - 1)
        return ((z + way * dz + NZ) % NZ) * NY + (y + way * dy + NY) % NY

    def slot_of(t):
        return table[t]

    def row_of(d):
        return table[N + d]

    def src_of(l):
        return table[2 * N + l]

    barrier = pltpu.get_barrier_semaphore()

    def greet(i, carry):
        pl.semaphore_signal(barrier, 1, device_id={"row": away(i, 1)}, device_id_type=MESH)
        return carry

    cut = ((), (pl.ds(0, H + 1),), ())

    def sent(phase, i, src, dst):
        t = away(i, 1)
        return pltpu.make_async_remote_copy(
            src.at[(t,) + cut[phase]], dst.at[(me,) + cut[phase]], a2a_send.at[phase, i], a2a_recv.at[phase, i],
            device_id={"row": t}, device_id_type=MESH,
        )

    def arriving(phase, i, src, dst):
        d = away(i, -1)
        return pltpu.make_async_remote_copy(
            src.at[(d,) + cut[phase]], dst.at[(d,) + cut[phase]], a2a_send.at[phase, i], a2a_recv.at[phase, i],
            device_id={"row": d}, device_id_type=MESH,
        )

    phases = ((sd_l, rc_l), (sd_d, rc_d), (sd_f, rc_f))
    owns = [
        pltpu.make_async_copy(src.at[me], dst.at[me], in_sem.at[3 + k]) for k, (src, dst) in enumerate(phases)
    ]

    def send_all(phase):
        src, dst = phases[phase]

        def start(i, carry):
            sent(phase, i, src, dst).start()
            return carry

        lax.fori_loop(1, N, start, 0)
        owns[phase].start()

    def receive_all(phase):
        src, dst = phases[phase]

        def wait(i, carry):
            arriving(phase, i, src, dst).wait_recv()
            return carry

        lax.fori_loop(1, N, wait, 0)
        owns[phase].wait()

    loads = [
        pltpu.make_async_copy(src, dst, in_sem.at[k])
        for k, (src, dst) in enumerate(((low_hbm, st_l), (diag_hbm, st_d), (rhs_hbm, st_f)))
    ]
    lax.fori_loop(1, N, greet, 0)
    for load in loads:
        load.start()
    loads[0].wait()

    def gather_l(t, carry):
        sd_l[t] = st_l[slot_of(t)]
        return carry

    def gather_d(t, carry):
        body, diagonal = triangle_of(st_d[slot_of(t)])
        sd_d[t, 0:H] = body
        sd_d[t, H:DROWS] = jnp.broadcast_to(diagonal, (8, B))
        return carry

    def gather_f(t, carry):
        sd_f[t] = st_f[slot_of(t)]
        return carry

    lax.fori_loop(0, N, gather_l, 0)
    pl.semaphore_wait(barrier, N - 1)
    send_all(0)
    loads[1].wait()
    lax.fori_loop(0, N, gather_d, 0)
    send_all(1)
    loads[2].wait()
    lax.fori_loop(0, N, gather_f, 0)
    send_all(2)

    base = me * BPD
    rows = iota((BPD, B), 0) + base
    lane = iota((BPD, B), 1)
    eighths = base + iota((BPD, 8 * BPD), 1) // 8
    cols = jnp.full((BPD, B), -1, jnp.int32)
    for k, j in enumerate((base - 1, base - BPD - 1, base + BPD, base + 2 * BPD)):
        cols = jnp.where(lane == k, j, cols)

    def count(q, carry):
        end, a, b, c, e = carry
        end = end + lengths[q]
        one = lambda m: jnp.where(m, 1, 0)
        return (
            end, a + one(rows >= end), b + one(cols >= end), c + one(rows - 1 >= end), e + one(eighths >= end),
        )

    zero = jnp.zeros((BPD, B), jnp.int32)
    _, seg, seg_cols, seg_before, seg_eighths = lax.fori_loop(
        0, SYSTEMS, count, (jnp.int32(0), zero, zero, zero, jnp.zeros((BPD, 8 * BPD), jnp.int32))
    )
    keep[...] = jnp.where((seg != seg_before) | (rows == 0), 0.0, 1.0)
    same = jnp.where((seg == seg_cols) & (cols >= 0), 1.0, 0.0).astype(F32)
    for k in range(4):
        near[k] = jnp.broadcast_to(same[:, k : k + 1], (BPD, B))
    same_here = jnp.where(jnp.concatenate([seg, seg], axis=1) == seg_eighths, 1.0, 0.0).astype(F32)

    def shift(by):
        return (me + by + N) % N

    def remote(src, dst, send, recv, by):
        return pltpu.make_async_remote_copy(
            src, dst, send, recv, device_id={"row": shift(by)}, device_id_type=MESH
        )

    receive_all(0)

    def open_l(d, carry):
        v = rc_l[d] * keep[pl.ds(row_of(d), 1)]
        w_l[d] = side(v)
        w_t[d] = side(v.T)
        return carry

    lax.fori_loop(0, N, open_l, 0)
    first_l[...] = rc_l[src_of(0)]
    couple = remote(first_l, next_l, halo_send.at[ITERS, 0], halo_recv.at[ITERS, 0], -1)
    couple.start()
    receive_all(1)

    def open_d(d, carry):
        w_d[d] = side(whole_of(rc_d[d, 0:H], rc_d[d, H : H + 1]))
        return carry

    lax.fori_loop(0, N, open_d, 0)
    couple.wait()
    w_n[...] = side(next_l[...].T)
    receive_all(2)

    def settle(l, carry):
        v = rc_f[src_of(l)]
        r[l] = v
        rw[l] = side(v)
        return carry

    lax.fori_loop(0, BPD, settle, 0)

    def swap(field, into, it):
        return [
            remote(field.at[row], into.at[k], halo_send.at[it, k], halo_recv.at[it, k], by)
            for k, (row, by) in enumerate(((BPD - 1, 1), (0, -1)))
        ]

    def joined(k, value):
        flag = near[0][0:1] if k == 0 else near[2][BPD - 1 : BPD]
        return jnp.where(flag > 0.0, value, 0.0)

    swap_f = swap(r, ends_f, ITERS - 1)
    for copy in swap_f:
        copy.start()

    def multiply(it):
        def products(j, kinds):
            here = src_of(j)
            mats = {"t": lambda: w_t[here], "d": lambda: w_d[here], "l": lambda: w_l[src_of(j + 1)]}
            out = times(jnp.concatenate([mats[kind]() for kind in kinds], axis=0), rw[j])
            return [out[k * B : (k + 1) * B] for k in range(len(kinds))]

        c, b = products(0, "dl")
        im[0] = c
        im[1] = b

        def step(j, carry):
            t, c, b = products(j, "tdl")
            im[j - 1] = im[j - 1] + t
            im[j] = im[j] + c
            im[j + 1] = b
            return carry

        lax.fori_loop(1, BPD - 1, step, 0)
        t, c = products(BPD - 1, "td")
        im[BPD - 2] = im[BPD - 2] + t
        if it == 0:
            for copy in swap_f:
                copy.wait()
            for k in range(2):
                v = joined(k, ends_f[k])
                ends_r[k] = v
                ends_rw[k] = side(v)
        im[0] = im[0] + times(w_l[src_of(0)], ends_rw[0])
        im[BPD - 1] = im[BPD - 1] + (c + times(w_n[...], ends_rw[1]))

    def two_sums(it):
        def row_sums(l, carry):
            v = r[l]
            at = pl.ds(pl.multiple_of(8 * l, 8), 8)
            ss_rows[at, 0:B] = jnp.sum((v * v).reshape(B // 8, 8, B), axis=0)
            ss_rows[at, B : 2 * B] = jnp.sum((v * im[l]).reshape(B // 8, 8, B), axis=0)
            return carry

        lax.fori_loop(0, BPD, row_sums, 0)
        local = jnp.dot(same_here, ss_rows[...], precision=HIGHEST, preferred_element_type=F32)
        for k, row in enumerate((0, BPD - 1)):
            part[it, k, 0:1] = local[row : row + 1, :B]
            part[it, k, 1:2] = local[row : row + 1, B:]
        copies = [
            remote(part.at[it, k], parts.at[it, q], part_send.at[it, q], part_recv.at[it, q], by)
            for q, (k, by) in enumerate(((1, 1), (1, 2), (0, -1), (0, -2)))
        ]
        for copy in copies:
            copy.start()
        first, second = local[:, :B], local[:, B:]
        for copy in copies:
            copy.wait_recv()
            copy.wait_send()
        for q in range(4):
            first = first + near[q] * parts[it, q, 0:1]
            second = second + near[q] * parts[it, q, 1:2]
        return first, second

    for it in range(ITERS):
        multiply(it)
        swap_im = swap(im, ends_im.at[it], it) if it + 1 < ITERS else []
        for copy in swap_im:
            copy.start()
        norm, product = two_sums(it)
        for copy in swap_im:
            copy.wait()
        if it == 0:
            step_size = norm / product
        else:
            ratio = norm / norm_before
            step_size = norm / (product - ratio * norm / step_size)
            beta[...] = ratio
        alpha[...] = step_size
        norm_before = norm

        def update(l, carry, it=it):
            a = alpha[pl.ds(l, 1)]
            res, image = r[l], im[l]
            if it == 0:
                direction, along = res, image
                x[l] = a * direction
            else:
                b = beta[pl.ds(l, 1)]
                direction = res + b * p[l]
                along = image + b * s[l]
                x[l] = x[l] + a * direction
            res = res - a * along
            r[l] = res
            p[l] = direction
            s[l] = along
            rw[l] = side(res)
            return carry

        if it + 1 < ITERS:
            lax.fori_loop(0, BPD, update, 0)
            for k, row in enumerate((0, BPD - 1)):
                along = joined(k, ends_im[it, k])
                if it > 0:
                    along = along + beta[row : row + 1] * ends_s[k]
                res = ends_r[k] - alpha[row : row + 1] * along
                ends_s[k] = along
                ends_r[k] = res
                ends_rw[k] = side(res)

    outs = []
    span = BPD // CHUNKS
    for c in range(CHUNKS):
        def finish(q, carry, c=c):
            l = c * span + q
            a = alpha[pl.ds(l, 1)]
            res, image = r[l], im[l]
            b = beta[pl.ds(l, 1)]
            x_out[c][q] = x[l] + a * (res + b * p[l])
            r_out[c][q] = res - a * (image + b * s[l])
            return carry

        lax.fori_loop(0, span, finish, 0)
        for k, (src, dst) in enumerate(((x_out, x_hbm), (r_out, r_hbm))):
            outs.append(pltpu.make_async_copy(src[c], dst.at[pl.ds(c * span, span)], out_sem.at[c, k]))
            outs[-1].start()

    def drained(i, carry):
        for phase, (src, dst) in enumerate(phases):
            sent(phase, i, src, dst).wait_send()
        return carry

    lax.fori_loop(1, N, drained, 0)
    for out in outs:
        out.wait()


def body(placing, lengths, diag_blocks, lower_blocks, right_side):
    me = lax.axis_index("row")
    slots = placing.reshape(N, BPD)
    owner, local = slots // BPD, slots % BPD
    index = jnp.arange(BPD, dtype=jnp.int32)
    own = lax.dynamic_slice_in_dim(owner, me, 1, 0)
    slot_of = jnp.sum(jnp.where(own == index[:, None], index[None, :], 0), axis=1)
    row_of = jnp.sum(jnp.where(owner == me, local, 0), axis=1)
    src_of = jnp.sum(
        jnp.where((owner == me) & (local == index[:, None, None]), index[None, :, None], 0), axis=(1, 2)
    )
    table = jnp.concatenate([slot_of, row_of, src_of]).astype(jnp.int32)
    field = jax.ShapeDtypeStruct((BPD, B, B), F32)
    smem, hbm = pl.BlockSpec(memory_space=pltpu.SMEM), pl.BlockSpec(memory_space=pl.ANY)
    blocks = pltpu.VMEM((BPD, B, B), F32)
    packed = pltpu.VMEM((BPD, DROWS, B), F32)
    pairs = pltpu.VMEM((BPD, B, 2 * B), BF16)
    lines = pltpu.VMEM((BPD, B), F32)
    pair = pltpu.VMEM((2, B, B), F32)
    block = pltpu.VMEM((B, B), F32)
    dma = pltpu.SemaphoreType.DMA
    return pl.pallas_call(
        kernel,
        out_shape=(field, field),
        in_specs=[smem, smem, hbm, hbm, hbm],
        out_specs=(hbm, hbm),
        scratch_shapes=[blocks] * 3 + [blocks, packed, blocks] * 2 + [pairs] * 3 + [blocks] * 5 + [pairs]
        + [pltpu.VMEM((8 * BPD, 2 * B), F32), lines, pltpu.VMEM((4, BPD, B), F32), lines, lines]
        + [pair, pltpu.VMEM((ITERS - 1, 2, B, B), F32), pair, pair, pltpu.VMEM((2, B, 2 * B), BF16), block, block]
        + [pltpu.VMEM((B, 2 * B), BF16), pltpu.VMEM((ITERS, 2, 8, B), F32), pltpu.VMEM((ITERS, 4, 8, B), F32)]
        + [(pltpu.VMEM((BPD // CHUNKS, B, B), F32),) * CHUNKS] * 2
        + [dma((6,)), dma((3, N)), dma((3, N)), dma((ITERS + 1, 2)), dma((ITERS + 1, 2)), dma((ITERS, 4)), dma((ITERS, 4)), dma((CHUNKS, 2))],
        compiler_params=pltpu.CompilerParams(
            collective_id=0, has_side_effects=True, vmem_limit_bytes=60 * 1024 * 1024
        ),
    )(table, lengths, right_side, diag_blocks, lower_blocks)


def solution(mesh):
    blocks = P(("grp", "row"), None, None)
    return jax.shard_map(
        body,
        mesh=mesh,
        in_specs=(P("grp"), P("grp"), blocks, blocks, blocks),
        out_specs=(blocks, blocks),
        check_vma=False,
    )
```
